256 devices in a mesh: dp: 8 (over z_hi, core), expert: 32 (over y, x, z_lo).
Axes of the slice: x: 4, y: 4, z: 8 (z_hi: 4, z_lo: 2; z = z_hi * 2 + z_lo), core: 2. Of those that a mesh axis runs over, the one named last changes fastest.
Arguments:
- tokens: bfloat16 [32768, 2048], P(('dp', 'expert')), may hold values from -6 to 6
- out_grad: bfloat16 [32768, 2048], P(('dp', 'expert')), may hold values from -3 to 3
- expert_ids: int32 [32768, 1], P(('dp', 'expert')), may hold values from 0 to 15, as said below
- gate_fixed: int32 [32768, 1], P(('dp', 'expert')), may hold values from 8192 to 65535
- w_gate: bfloat16 [32, 2048, 384], P('expert', 'dp'), may hold values from -0.125 to 0.125
- w_up: bfloat16 [32, 2048, 384], P('expert', 'dp'), may hold values from -0.125 to 0.125
- w_down: bfloat16 [32, 384, 2048], P('expert', None, 'dp'), may hold values from -0.21875 to 0.21875
- m_gate: float32 [32, 2048, 384], P('expert', 'dp'), may hold values from -12 to 12
- m_up: float32 [32, 2048, 384], P('expert', 'dp'), may hold values from -12 to 12
- m_down: float32 [32, 384, 2048], P('expert', None, 'dp'), may hold values from -12 to 12
- v_gate: float32 [32, 2048, 384], P('expert', 'dp'), may hold values from 1 to 100
- v_up: float32 [32, 2048, 384], P('expert', 'dp'), may hold values from 1 to 100
- v_down: float32 [32, 384, 2048], P('expert', None, 'dp'), may hold values from 1 to 100
Outputs:
- input_grad: bfloat16 [32768, 2048], P(('dp', 'expert'))
- new_w_gate: bfloat16 [32, 2048, 384], P('expert', 'dp')
- new_w_up: bfloat16 [32, 2048, 384], P('expert', 'dp')
- new_w_down: bfloat16 [32, 384, 2048], P('expert', None, 'dp')
- new_m_gate: float32 [32, 2048, 384], P('expert', 'dp')
- new_m_up: float32 [32, 2048, 384], P('expert', 'dp')
- new_m_down: float32 [32, 384, 2048], P('expert', None, 'dp')
- new_v_gate: float32 [32, 2048, 384], P('expert', 'dp')
- new_v_up: float32 [32, 2048, 384], P('expert', 'dp')
- new_v_down: float32 [32, 384, 2048], P('expert', None, 'dp')
The draws below stay inside these ranges and needn't reach their ends.
Inputs may be any that keep to these rules, and one draw needn't show every extreme that they name: `expert_ids`: in each aligned block of 128 tokens (the tokens of one device) one expert, the same in every block, is named exactly 32 times; every other expert is named at most 8 times, and some other expert exactly 8 times in every block.
All inputs are finite; a program needn't handle non-finite values.
Results may differ from the reference program's by a relative error of at most 0.024.
Values may be sent and summed in bfloat16 or wider, within the bound.
No kernel may reach another device: no remote copies, remote signals or barrier semaphores. Data moves between devices by JAX's collectives and lax.ppermute only.
A program may use at most 128 MiB of HBM per device.

```python
import math
import jax
import jax.numpy as jnp
from jax import lax

D = 2048
FF = 768
TOK_DEV = 128
HALF = 384
EXPERTS = 16
CAP = 8
HOT = 32
TOKENS = 32768


def draw_expert_ids(key, part):
    blocks = TOKENS // TOK_DEV
    hot_key, rest_key = jax.random.split(jax.random.fold_in(key, 11))
    hottest = jax.random.randint(hot_key, (), 0, EXPERTS).astype(jnp.int32)

    def one_block(block_index):
        block_key = jax.random.fold_in(rest_key, block_index)
        second_key, pick_key, place_key = jax.random.split(block_key, 3)
        second = ((hottest + 1 + jax.random.randint(second_key, (), 0, EXPERTS - 1)) % EXPERTS).astype(jnp.int32)
        low_pick = jnp.minimum(hottest, second)
        high_pick = jnp.maximum(hottest, second)
        places = jax.random.permutation(pick_key, (EXPERTS - 2) * CAP)[:TOK_DEV - HOT - CAP]
        others = (places // CAP).astype(jnp.int32)
        others = others + (others >= low_pick).astype(jnp.int32)
        others = others + (others >= high_pick).astype(jnp.int32)
        labels = jnp.concatenate([jnp.full((HOT,), hottest, jnp.int32), jnp.full((CAP,), second, jnp.int32), others])
        shuffle = jax.random.permutation(place_key, TOK_DEV)
        return labels[shuffle]
    labels = jax.vmap(one_block)(jnp.arange(blocks, dtype=jnp.int32))
    return labels.reshape(TOKENS, 1).astype(jnp.int32)


def set_ends(values, rng, smallest, high):
    index_at = [jax.random.randint(jax.random.fold_in(rng, axis), (), 0, length) for axis, length in enumerate(values.shape)]
    widest = values.shape.index(max(values.shape))
    neighbour = index_at[:widest] + [(index_at[widest] + 1) % values.shape[widest]] + index_at[widest + 1:]
    return values.at[tuple(index_at)].set(smallest).at[tuple(neighbour)].set(high)


def level_of(key, shape, shards, least, largest):
    factor_of = 1.0
    for axis_at, parts in shards:
        heights = jax.random.uniform(jax.random.fold_in(jax.random.fold_in(key, 6), axis_at), (parts,), jnp.float32, least / len(shards), largest / len(shards))
        factor_of = factor_of * jnp.repeat(jnp.exp(heights), shape[axis_at] // parts).reshape((-1,) + (1,) * (len(shape) - 1 - axis_at))
    return factor_of


def normal_values(key, shape, deviation, reach, shards=(), kind=jnp.bfloat16):
    result = deviation * jax.random.normal(key, shape, jnp.float32)
    if shards:
        result = result * level_of(key, shape, shards, -0.22, 0.18)
    return jnp.clip(result, -reach, reach).astype(kind)


def setup_inputs(seed: int = 0) -> dict:
    key_of = jax.random.split(jax.random.key(seed), 14)
    return {
        "tokens": normal_values(key_of[0], (TOKENS, D), 1.0, 6.0, ((0, 256),)),
        "out_grad": normal_values(key_of[1], (TOKENS, D), 0.5, 3.0, ((0, 256),)),
        "expert_ids": draw_expert_ids(jax.random.fold_in(key_of[13], 71), 0),
        "gate_fixed": set_ends(jax.random.randint(key_of[3], (TOKENS, 1), 8192, 65536), jax.random.fold_in(key_of[3], 1), 8192, 65535).astype(jnp.int32),
        "w_gate": normal_values(key_of[4], (2 * EXPERTS, D, HALF), D ** -0.5, 0.125, ((0, 32), (1, 8))),
        "w_up": normal_values(key_of[5], (2 * EXPERTS, D, HALF), D ** -0.5, 0.125, ((0, 32), (1, 8))),
        "w_down": normal_values(key_of[6], (2 * EXPERTS, HALF, D), FF ** -0.5, 0.21875, ((0, 32), (2, 8))),
        "m_gate": normal_values(key_of[7], (2 * EXPERTS, D, HALF), 2.0, 12.0, ((0, 32), (1, 8)), jnp.float32),
        "m_up": normal_values(key_of[8], (2 * EXPERTS, D, HALF), 2.0, 12.0, ((0, 32), (1, 8)), jnp.float32),
        "m_down": normal_values(key_of[9], (2 * EXPERTS, HALF, D), 2.0, 12.0, ((0, 32), (2, 8)), jnp.float32),
        "v_gate": jnp.clip(jnp.exp(math.log(100.0) - 4.6051702 * jax.random.uniform(key_of[10], (2 * EXPERTS, D, HALF), jnp.float32) ** level_of(key_of[10], (2 * EXPERTS, D, HALF), ((0, 32), (1, 8)), -0.2, 0.2)), 1.0, 100.0),
        "v_up": jnp.clip(jnp.exp(math.log(100.0) - 4.6051702 * jax.random.uniform(key_of[11], (2 * EXPERTS, D, HALF), jnp.float32) ** level_of(key_of[11], (2 * EXPERTS, D, HALF), ((0, 32), (1, 8)), -0.2, 0.2)), 1.0, 100.0),
        "v_down": jnp.clip(jnp.exp(math.log(100.0) - 4.6051702 * jax.random.uniform(key_of[12], (2 * EXPERTS, HALF, D), jnp.float32) ** level_of(key_of[12], (2 * EXPERTS, HALF, D), ((0, 32), (2, 8)), -0.2, 0.2)), 1.0, 100.0),
    }


beta_one = 0.9
beta_two = 0.95
learn_rate = 0.002
decay_rate = 0.1
epsilon = 1e-08
bias_one = 1.0 - beta_one ** 20
bias_two = 1.0 - beta_two ** 20
fixed_scale = 1.0 / 65536.0
block_rows = 256

def expert_block(rows_input, rows_cotangent, gate_full, up_full, down_full):
    gate_pre = jnp.dot(rows_input, gate_full, preferred_element_type=jnp.float32)
    up_pre = jnp.dot(rows_input, up_full, preferred_element_type=jnp.float32)
    sigmoid_gate = jax.nn.sigmoid(gate_pre)
    active = gate_pre * sigmoid_gate
    hidden = (active * up_pre).astype(jnp.bfloat16)
    hidden_cot = jnp.dot(rows_cotangent, down_full.T, preferred_element_type=jnp.float32)
    grad_up = (hidden_cot * active).astype(jnp.bfloat16)
    grad_gate = (hidden_cot * up_pre * sigmoid_gate * (1.0 + gate_pre * (1.0 - sigmoid_gate))).astype(jnp.bfloat16)
    row_grad = jnp.dot(grad_gate, gate_full.T, preferred_element_type=jnp.float32) + jnp.dot(grad_up, up_full.T, preferred_element_type=jnp.float32)
    return (hidden, grad_gate, grad_up, row_grad)

def adam_update(weight, gradient, moment_one, moment_two):
    weight_full = weight.astype(jnp.float32)
    first_new = beta_one * moment_one + (1.0 - beta_one) * gradient
    second_new = beta_two * moment_two + (1.0 - beta_two) * gradient * gradient
    update = first_new / bias_one / (jnp.sqrt(second_new / bias_two) + epsilon) + decay_rate * weight_full
    return ((weight_full - learn_rate * update).astype(jnp.bfloat16), first_new, second_new)

def pair_join(array, expert, axis_index):
    pair_rows = lax.dynamic_slice_in_dim(array, 2 * expert, 2, 0)
    return jnp.concatenate([pair_rows[0], pair_rows[1]], axis=axis_index)

def pair_split(array, axis_index):
    halves = jnp.split(array, 2, axis=axis_index)
    return jnp.stack(halves)

def reference(tokens, out_grad, expert_ids, gate_fixed, w_gate, w_up, w_down, m_gate, m_up, m_down, v_gate, v_up, v_down):
    token_scale = gate_fixed[:, 0].astype(jnp.float32) * fixed_scale
    cotangent = (out_grad.astype(jnp.float32) * token_scale[:, None]).astype(jnp.bfloat16)
    chosen = expert_ids[:, 0].astype(jnp.int32)
    sorted_rows = jnp.argsort(chosen, stable=True).astype(jnp.int32)
    counts = jax.ops.segment_sum(jnp.ones((TOKENS,), jnp.int32), chosen, num_segments=EXPERTS).astype(jnp.int32)
    starts = (jnp.cumsum(counts) - counts).astype(jnp.int32)
    sorted_pad = jnp.concatenate([sorted_rows, jnp.full((block_rows,), TOKENS, jnp.int32)])
    input_pad = jnp.concatenate([tokens, jnp.zeros((1, D), tokens.dtype)], axis=0)
    cotangent_pad = jnp.concatenate([cotangent, jnp.zeros((1, D), cotangent.dtype)], axis=0)

    def per_expert(grad_rows, expert):
        gate_full = pair_join(w_gate, expert, 1)
        up_full = pair_join(w_up, expert, 1)
        down_full = pair_join(w_down, expert, 0)
        first_row = starts[expert]
        row_count = counts[expert]
        block_count = ((row_count + block_rows - 1) // block_rows).astype(jnp.int32)

        def per_block(block_index, block_state):
            grad_rows, gate_part, up_part, down_part = block_state
            positions = (first_row + block_index * block_rows + jnp.arange(block_rows, dtype=jnp.int32)).astype(jnp.int32)
            in_group = positions < first_row + row_count
            row_index = jnp.where(in_group, jnp.take(sorted_pad, positions), TOKENS).astype(jnp.int32)
            rows_input = jnp.take(input_pad, row_index, axis=0)
            rows_cotangent = jnp.take(cotangent_pad, row_index, axis=0)
            hidden, grad_gate, grad_up, row_grad = expert_block(rows_input, rows_cotangent, gate_full, up_full, down_full)
            gate_part = gate_part + jnp.dot(rows_input.T, grad_gate, preferred_element_type=jnp.float32)
            up_part = up_part + jnp.dot(rows_input.T, grad_up, preferred_element_type=jnp.float32)
            down_part = down_part + jnp.dot(hidden.T, rows_cotangent, preferred_element_type=jnp.float32)
            grad_rows = grad_rows.at[row_index].set(row_grad.astype(jnp.bfloat16))
            return (grad_rows, gate_part, up_part, down_part)
        zero_in = jnp.zeros((D, FF), jnp.float32)
        zero_out = jnp.zeros((FF, D), jnp.float32)
        grad_rows, gate_total, up_total, down_total = lax.fori_loop(jnp.int32(0), block_count, per_block, (grad_rows, zero_in, zero_in, zero_out))
        gate_new, gate_first, gate_second = adam_update(gate_full, gate_total, pair_join(m_gate, expert, 1), pair_join(v_gate, expert, 1))
        up_new, up_first, up_second = adam_update(up_full, up_total, pair_join(m_up, expert, 1), pair_join(v_up, expert, 1))
        down_new, down_first, down_second = adam_update(down_full, down_total, pair_join(m_down, expert, 0), pair_join(v_down, expert, 0))
        results = (pair_split(gate_new, 1), pair_split(up_new, 1), pair_split(down_new, 0), pair_split(gate_first, 1), pair_split(up_first, 1), pair_split(down_first, 0), pair_split(gate_second, 1), pair_split(up_second, 1), pair_split(down_second, 0))
        return (grad_rows, results)
    grad_init = jnp.zeros((TOKENS + 1, D), jnp.bfloat16)
    grad_rows, stacked = lax.scan(per_expert, grad_init, jnp.arange(EXPERTS, dtype=jnp.int32))
    flat = [jnp.reshape(item, (2 * EXPERTS,) + item.shape[2:]) for item in stacked]
    return (grad_rows[:TOKENS], flat[0], flat[1], flat[2], flat[3], flat[4], flat[5], flat[6], flat[7], flat[8])
```

```python
import functools

import jax
import jax.numpy as jnp
from jax import lax
from jax.experimental import pallas as pl
from jax.experimental.pallas import tpu as pltpu
from jax.sharding import Mesh
from jax.sharding import PartitionSpec as P


beta_one = 0.9
beta_two = 0.95
learn_rate = 0.002
decay_rate = 0.1
epsilon = 1e-08
bias_one = 1.0 - beta_one**20
bias_two = 1.0 - beta_two**20
fixed_scale = 1.0 / 65536.0

f32 = jnp.float32
bf16 = jnp.bfloat16
ROWS = 32
SIDE = 4
RING = 8
COLS = SIDE * SIDE
REACH = (4, 3, 4)
VMEM_LIMIT = 56 * 1024 * 1024

contract_last = (((1,), (1,)), ((), ()))
contract_first = (((0,), (0,)), ((), ()))


def dot(a, b, dims=(((1,), (0,)), ((), ()))):
    return lax.dot_general(a, b, dims, preferred_element_type=f32)


def vmem_specs(n):
    return [pl.BlockSpec(memory_space=pltpu.VMEM)] * n


def smem_spec():
    return pl.BlockSpec(memory_space=pltpu.SMEM)


def params():
    return pltpu.CompilerParams(vmem_limit_bytes=VMEM_LIMIT)


def up_z(v):
    return lax.ppermute(v, ("zh", "zl"), [(i, (i + 1) % RING) for i in range(RING)])


def down_z(v):
    return lax.ppermute(v, ("zh", "zl"), [(i, (i - 1) % RING) for i in range(RING)])


def swap_core(v):
    return lax.ppermute(v, "c", [(0, 1), (1, 0)])


def shift_column(v, k, back=False):
    if k == 0:
        return v
    dy, dx = divmod(k, SIDE)
    pairs = []
    for y in range(SIDE):
        for x in range(SIDE):
            there = ((y + dy) % SIDE) * SIDE + (x + dx) % SIDE
            here = y * SIDE + x
            pairs.append((there, here) if back else (here, there))
    return lax.ppermute(v, ("y", "x"), pairs)


def dispatch_body(place, ids_ref, gate_ref, tok_ref, grad_ref, pick_ref, *outs):
    rows = ids_ref.shape[1]
    ids = ids_ref[...]
    onehot = ids == lax.broadcasted_iota(jnp.int32, (COLS, rows), 0)
    ones = jnp.where(onehot, 1.0, 0.0)
    before = lax.broadcasted_iota(jnp.int32, (rows, rows), 0) <= lax.broadcasted_iota(
        jnp.int32, (rows, rows), 1
    )
    count = dot(ones.astype(bf16), jnp.where(before, 1.0, 0.0).astype(bf16))
    position = jnp.sum(ones * count, axis=0, keepdims=True).astype(jnp.int32) - 1
    dy = (lax.shift_right_logical(ids, 2) - place[0]) & 3
    dx = ((ids & 3) - place[1]) & 3
    slot = (dy * SIDE + dx) * ROWS + position
    pick = jnp.where(
        lax.broadcasted_iota(jnp.int32, (COLS * ROWS, rows), 0) == slot, 1.0, 0.0
    ).astype(bf16)
    pick_ref[...] = pick
    scale = gate_ref[...].astype(f32) * fixed_scale
    tok = tok_ref[...]
    cot = (grad_ref[...].astype(f32) * scale).astype(bf16)
    for q in range(4):
        part = pick[q * 128 : (q + 1) * 128]
        a = dot(part, tok).astype(bf16)
        b = dot(part, cot).astype(bf16)
        for i in range(4):
            outs[q * 4 + i][0:ROWS] = a[i * ROWS : (i + 1) * ROWS]
            outs[q * 4 + i][ROWS : 2 * ROWS] = b[i * ROWS : (i + 1) * ROWS]


def dispatch(place, ids, gate, tokens, out_grad):
    rows, width = tokens.shape
    return pl.pallas_call(
        dispatch_body,
        out_shape=[jax.ShapeDtypeStruct((COLS * ROWS, rows), bf16)]
        + [jax.ShapeDtypeStruct((2 * ROWS, width), bf16)] * COLS,
        in_specs=[smem_spec()] + vmem_specs(4),
        out_specs=vmem_specs(1 + COLS),
        compiler_params=params(),
        name="dispatch",
    )(place, ids, gate, tokens, out_grad)


def combine_body(pick_ref, *refs):
    out = refs[-1]
    total = None
    for q in range(4):
        rows = jnp.concatenate([refs[q * 4 + i][...] for i in range(4)], axis=0)
        part = dot(pick_ref[q * 128 : (q + 1) * 128, :], rows, contract_first)
        total = part if total is None else total + part
    out[...] = total.astype(bf16)


def combine(pick, pieces):
    return pl.pallas_call(
        combine_body,
        out_shape=jax.ShapeDtypeStruct((pick.shape[1], pieces[0].shape[1]), bf16),
        in_specs=vmem_specs(1 + COLS),
        out_specs=pl.BlockSpec(memory_space=pltpu.VMEM),
        compiler_params=params(),
        name="combine",
    )(pick, *pieces)


def forward_body(table, *refs):
    got = refs[:COLS]
    gates = refs[COLS : COLS + 16]
    ups = refs[COLS + 16 : COLS + 32]
    downs = refs[COLS + 32 : COLS + 48]
    tok_ref, cot_ref, cat_ref, turn_ref, pre_acc, cot_acc = refs[COLS + 48 :]
    slices, rows, width = tok_ref.shape
    half = cot_acc.shape[2]
    for d in range(slices):
        lanes = slice(d * width, (d + 1) * width)
        for i in range(COLS):
            tok_ref[d, i * ROWS : (i + 1) * ROWS, :] = got[i][0:ROWS, lanes]
            cot_ref[d, i * ROWS : (i + 1) * ROWS, :] = got[i][ROWS : 2 * ROWS, lanes]
    for r in range(2):
        for n, k in enumerate(range(r, RING, 2)):
            at = table[2 * k]
            to = table[2 * k + 1]
            tok_a, tok_b = tok_ref[at], tok_ref[to]
            cot_a, cot_b = cot_ref[at], cot_ref[to]
            pre = dot(
                tok_a, jnp.concatenate([gates[2 * k][...], ups[2 * k][...]], axis=1)
            ) + dot(
                tok_b, jnp.concatenate([gates[2 * k + 1][...], ups[2 * k + 1][...]], axis=1)
            )
            hid = dot(cot_a, downs[2 * k][...], contract_last) + dot(
                cot_b, downs[2 * k + 1][...], contract_last
            )
            if n == 0:
                pre_acc[...] = pre
                cot_acc[r] = hid
            else:
                pre_acc[...] += pre
                cot_acc[r] += hid
        for b in range(0, rows, 128):
            g = pre_acc[b : b + 128, 0:half]
            u = pre_acc[b : b + 128, half : 2 * half]
            h = cot_acc[r, b : b + 128, :]
            sig = jax.nn.sigmoid(g)
            act = g * sig
            hidden = (act * u).astype(bf16)
            grad_up = (h * act).astype(bf16)
            grad_gate = (h * u * sig * (1.0 + g * (1.0 - sig))).astype(bf16)
            cat_ref[r, b : b + 128, 0:half] = grad_gate
            cat_ref[r, b : b + 128, half : 2 * half] = grad_up
            turn_ref[r, 0:half, b : b + 128] = grad_gate.T
            turn_ref[r, half : 2 * half, b : b + 128] = grad_up.T
            turn_ref[r, 2 * half : 3 * half, b : b + 128] = hidden.T


def forward(table, got, gates, ups, downs):
    width, half = gates[0].shape
    rows = COLS * ROWS
    return pl.pallas_call(
        forward_body,
        out_shape=[
            jax.ShapeDtypeStruct((RING, rows, width), bf16),
            jax.ShapeDtypeStruct((RING, rows, width), bf16),
            jax.ShapeDtypeStruct((2, rows, 2 * half), bf16),
            jax.ShapeDtypeStruct((2, 3 * half, rows), bf16),
        ],
        in_specs=[smem_spec()] + vmem_specs(COLS + 48),
        out_specs=vmem_specs(4),
        scratch_shapes=[
            pltpu.VMEM((rows, 2 * half), f32),
            pltpu.VMEM((2, rows, half), f32),
        ],
        compiler_params=params(),
        name="forward",
    )(table, *got, *gates, *ups, *downs)


def rows_body(table, cat_ref, *refs):
    gates = refs[:16]
    ups = refs[16:32]
    outs = refs[32 : 32 + COLS]
    acc = refs[32 + COLS]
    width = acc.shape[2]
    for r in range(2):
        for k in range(r, RING, 2):
            for j in range(2):
                n = 2 * k + j
                part = dot(
                    cat_ref[r],
                    jnp.concatenate([gates[n][...], ups[n][...]], axis=1),
                    contract_last,
                )
                if r == 0:
                    acc[table[n]] = part
                else:
                    acc[table[n]] += part
    for d in range(acc.shape[0]):
        for i in range(COLS):
            outs[i][:, d * width : (d + 1) * width] = acc[d, i * ROWS : (i + 1) * ROWS, :].astype(
                bf16
            )


def row_grads(table, cat, gates, ups):
    width = gates[0].shape[0]
    return pl.pallas_call(
        rows_body,
        out_shape=[jax.ShapeDtypeStruct((ROWS, RING * width), bf16)] * COLS,
        in_specs=[smem_spec()] + vmem_specs(33),
        out_specs=vmem_specs(COLS),
        scratch_shapes=[pltpu.VMEM((RING, cat.shape[1], width), f32)],
        compiler_params=params(),
        name="row_grads",
    )(table, cat, *gates, *ups)


def terms_body(table, turn_ref, tok_a, tok_b, cot_a, cot_b, *outs):
    half = outs[0].shape[0]
    for j, (tok, cot) in enumerate(((tok_a, cot_a), (tok_b, cot_b))):
        both = dot(turn_ref[0, 0 : 2 * half, :], tok[0]).astype(bf16)
        outs[3 * j][...] = both[0:half]
        outs[3 * j + 1][...] = both[half : 2 * half]
        outs[3 * j + 2][...] = dot(turn_ref[0, 2 * half : 3 * half, :], cot[0]).astype(bf16)


def weight_terms(table, turn, tok, cot, k):
    _, triple, rows = turn.shape
    width = tok.shape[2]
    half = triple // 3
    at = [pl.BlockSpec((1, rows, width), lambda g, t, n=2 * k + j: (t[n], 0, 0)) for j in range(2)]
    return pl.pallas_call(
        terms_body,
        out_shape=[jax.ShapeDtypeStruct((half, width), bf16)] * 6,
        grid_spec=pltpu.PrefetchScalarGridSpec(
            num_scalar_prefetch=1,
            grid=(1,),
            in_specs=[pl.BlockSpec((1, triple, rows), lambda g, t: (k % 2, 0, 0))] + at + at,
            out_specs=[pl.BlockSpec((half, width), lambda g, t: (0, 0))] * 6,
        ),
        compiler_params=params(),
        name="weight_terms",
    )(table, turn, tok, tok, cot, cot)


def adam_body(turned, a, b, c, d, w_ref, m_ref, v_ref, w_out, m_out, v_out):
    gradient = (
        a[...].astype(f32) + b[...].astype(f32) + c[...].astype(f32) + d[...].astype(f32)
    )
    if turned:
        gradient = gradient.T
    weight = w_ref[0].astype(f32)
    first = beta_one * m_ref[0] + (1.0 - beta_one) * gradient
    second = beta_two * v_ref[0] + (1.0 - beta_two) * gradient * gradient
    update = (
        first / bias_one / (jnp.sqrt(second / bias_two) + epsilon) + decay_rate * weight
    )
    w_out[0] = (weight - learn_rate * update).astype(bf16)
    m_out[0] = first
    v_out[0] = second


def adam(turned, parts, weight, first, second):
    return pl.pallas_call(
        functools.partial(adam_body, turned),
        out_shape=[
            jax.ShapeDtypeStruct(weight.shape, bf16),
            jax.ShapeDtypeStruct(weight.shape, f32),
            jax.ShapeDtypeStruct(weight.shape, f32),
        ],
        in_specs=vmem_specs(7),
        out_specs=vmem_specs(3),
        compiler_params=params(),
        name="adam",
    )(*parts, weight, first, second)


def gather_ring(own, reach):
    chunks = [None] * RING
    chunks[0] = own
    rising, falling = own, own
    for step in range(1, reach + 1):
        rising = up_z(rising)
        chunks[RING - step] = rising
        if step <= RING - 1 - reach:
            falling = down_z(falling)
            chunks[step] = falling
    for step in range(reach + 1, RING - reach):
        falling = down_z(falling)
        chunks[step] = falling
    return [v for chunk in chunks for v in (chunk, swap_core(chunk))]


def ring_sum(mine, theirs, carried=None):
    total = mine.astype(f32) + theirs.astype(f32)
    if carried is not None:
        total = total + carried.astype(f32)
    return total.astype(bf16)


def scatter_ring(own, other, reach):
    rising = ring_sum(own[reach], other[reach])
    for k in range(reach - 1, -1, -1):
        rising = up_z(rising)
        if k:
            rising = ring_sum(own[k], other[k], rising)
    fall = RING - 1 - reach
    falling = ring_sum(own[RING - fall], other[RING - fall])
    for k in range(fall - 1, -1, -1):
        falling = down_z(falling)
        if k:
            falling = ring_sum(own[RING - k], other[RING - k], falling)
    return own[0], other[0], rising, falling


def per_device(
    tokens,
    out_grad,
    expert_ids,
    gate_fixed,
    w_gate,
    w_up,
    w_down,
    m_gate,
    m_up,
    m_down,
    v_gate,
    v_up,
    v_down,
):
    zh, zl, core = lax.axis_index("zh"), lax.axis_index("zl"), lax.axis_index("c")
    place = jnp.stack([lax.axis_index("y"), lax.axis_index("x")]).astype(jnp.int32)
    step = jnp.arange(RING, dtype=jnp.int32)[:, None]
    chip = (zh * 2 + zl + step) % RING
    side = jnp.bitwise_xor(core, jnp.arange(2, dtype=jnp.int32)[None, :])
    table = ((chip // 2) * 2 + side).reshape(2 * RING).astype(jnp.int32)

    picked = dispatch(
        place, expert_ids.reshape(1, tokens.shape[0]), gate_fixed, tokens, out_grad
    )
    pick, sent = picked[0], picked[1:]
    gates = gather_ring(w_gate[0], REACH[0])
    ups = gather_ring(w_up[0], REACH[1])
    downs = gather_ring(w_down[0], REACH[2])
    got = [shift_column(v, k) for k, v in enumerate(sent)]
    tok, cot, cat, turn = forward(table, got, gates, ups, downs)

    pieces = row_grads(table, cat, gates, ups)
    back = [shift_column(v, k, back=True) for k, v in enumerate(pieces)]
    input_grad = combine(pick, back)

    own = [[None] * RING for _ in range(3)]
    other = [[None] * RING for _ in range(3)]
    for k in (4, 3, 5, 2, 6, 1, 7, 0):
        terms = weight_terms(table, turn, tok, cot, k)
        for m in range(3):
            own[m][k] = terms[m]
            other[m][k] = swap_core(terms[3 + m])
    results = []
    for m, (weight, first, second) in enumerate(
        ((w_gate, m_gate, v_gate), (w_up, m_up, v_up), (w_down, m_down, v_down))
    ):
        parts = scatter_ring(own[m], other[m], REACH[m])
        results.append(adam(m < 2, parts, weight, first, second))
    return (input_grad,) + tuple(results[m][i] for i in range(3) for m in range(3))


def solution(mesh):
    fine = Mesh(mesh.devices.reshape(4, 2, SIDE, SIDE, 2), ("zh", "c", "y", "x", "zl"))
    rows = P(("zh", "c", "y", "x", "zl"), None)
    tall = P(("y", "x", "zl"), ("zh", "c"), None)
    wide = P(("y", "x", "zl"), None, ("zh", "c"))
    states = (tall, tall, wide)
    return jax.shard_map(
        per_device,
        mesh=fine,
        in_specs=(rows,) * 4 + states * 3,
        out_specs=(rows,) + states * 3,
        check_vma=False,
    )
```

```python
import functools

import jax
import jax.numpy as jnp
from jax import lax
from jax.experimental import pallas as pl
from jax.experimental.pallas import tpu as pltpu
from jax.sharding import Mesh
from jax.sharding import PartitionSpec as P


beta_one = 0.9
beta_two = 0.95
learn_rate = 0.002
decay_rate = 0.1
epsilon = 1e-08
bias_one = 1.0 - beta_one**20
bias_two = 1.0 - beta_two**20
fixed_scale = 1.0 / 65536.0

f32 = jnp.float32
bf16 = jnp.bfloat16
ROWS = 32
SIDE = 4
RING = 8
COLS = SIDE * SIDE
REACH = (4, 3)
VMEM_LIMIT = 56 * 1024 * 1024

contract_last = (((1,), (1,)), ((), ()))
contract_first = (((0,), (0,)), ((), ()))


def dot(a, b, dims=(((1,), (0,)), ((), ()))):
    return lax.dot_general(a, b, dims, preferred_element_type=f32)


def vmem_specs(n):
    return [pl.BlockSpec(memory_space=pltpu.VMEM)] * n


def smem_spec():
    return pl.BlockSpec(memory_space=pltpu.SMEM)


def params():
    return pltpu.CompilerParams(vmem_limit_bytes=VMEM_LIMIT)


def up_z(v):
    return lax.ppermute(v, ("zh", "zl"), [(i, (i + 1) % RING) for i in range(RING)])


def down_z(v):
    return lax.ppermute(v, ("zh", "zl"), [(i, (i - 1) % RING) for i in range(RING)])


def swap_core(v):
    return lax.ppermute(v, "c", [(0, 1), (1, 0)])


def columns(v):
    return lax.all_to_all(v, ("y", "x"), split_axis=0, concat_axis=0, tiled=True)


def dispatch_body(ids_ref, gate_ref, tok_ref, grad_ref, pick_ref, out_ref):
    rows = ids_ref.shape[1]
    ids = ids_ref[...]
    first = lax.broadcasted_iota(jnp.int32, (rows, rows), 0)
    second = lax.broadcasted_iota(jnp.int32, (rows, rows), 1)
    ones = jnp.where(ids == lax.broadcasted_iota(jnp.int32, (COLS, rows), 0), 1.0, 0.0)
    count = dot(ones.astype(bf16), jnp.where(first <= second, 1.0, 0.0).astype(bf16))
    position = jnp.sum(ones * count, axis=0, keepdims=True).astype(jnp.int32) - 1
    slot = ids * ROWS + position
    pick = jnp.where(
        lax.broadcasted_iota(jnp.int32, (COLS * ROWS, rows), 0) == slot, 1.0, 0.0
    ).astype(bf16)
    pick_ref[...] = pick
    scale_row = gate_ref[...].astype(f32) * fixed_scale
    scale = jnp.sum(jnp.where(first == second, scale_row, 0.0), axis=1, keepdims=True)
    tok = tok_ref[...]
    cot = (grad_ref[...].astype(f32) * scale).astype(bf16)
    width = out_ref.shape[3]
    for n, source in enumerate((tok, cot)):
        for d in range(out_ref.shape[1]):
            part = dot(pick, source[:, d * width : (d + 1) * width])
            out_ref[:, d, n * ROWS : (n + 1) * ROWS, :] = part.astype(bf16).reshape(
                COLS, ROWS, width
            )


def dispatch(ids, gate, tokens, out_grad):
    rows, width = tokens.shape
    sent = jax.ShapeDtypeStruct((COLS, RING, 2 * ROWS, width // RING), bf16)
    return pl.pallas_call(
        dispatch_body,
        out_shape=[jax.ShapeDtypeStruct((COLS * ROWS, rows), bf16), sent],
        in_specs=vmem_specs(4),
        out_specs=vmem_specs(2),
        compiler_params=params(),
        name="dispatch",
    )(ids, gate, tokens, out_grad)


def slice_of(ref, d, n=0):
    return ref[:, d, n * ROWS : (n + 1) * ROWS, :].reshape(COLS * ROWS, ref.shape[3])


def combine_body(pick_ref, back_ref, out_ref):
    width = back_ref.shape[3]
    for d in range(back_ref.shape[1]):
        part = dot(pick_ref[...], slice_of(back_ref, d), contract_first)
        out_ref[:, d * width : (d + 1) * width] = part.astype(bf16)


def combine(pick, back):
    return pl.pallas_call(
        combine_body,
        out_shape=jax.ShapeDtypeStruct((pick.shape[1], back.shape[1] * back.shape[3]), bf16),
        in_specs=vmem_specs(2),
        out_specs=pl.BlockSpec(memory_space=pltpu.VMEM),
        compiler_params=params(),
        name="combine",
    )(pick, back)


def side_by_side(pair):
    return jnp.concatenate([pair[0], pair[1]], axis=1)


def forward_body(table, got, *refs):
    pairs = refs[:16]
    downs = refs[16:32]
    cat_ref, turn_ref, pre_acc, cot_acc = refs[32:]
    rows, half = cot_acc.shape
    for r in range(2):
        for k in range(r, RING, 2):
            at, to = 2 * k, 2 * k + 1
            pre = dot(slice_of(got, table[at]), side_by_side(pairs[at])) + dot(
                slice_of(got, table[to]), side_by_side(pairs[to])
            )
            hid = dot(slice_of(got, table[at], 1), downs[at][...], contract_last) + dot(
                slice_of(got, table[to], 1), downs[to][...], contract_last
            )
            if k == r:
                pre_acc[...] = pre
                cot_acc[...] = hid
            else:
                pre_acc[...] += pre
                cot_acc[...] += hid
        for b in range(0, rows, 128):
            g = pre_acc[b : b + 128, 0:half]
            u = pre_acc[b : b + 128, half : 2 * half]
            h = cot_acc[b : b + 128, :]
            sig = jax.nn.sigmoid(g)
            act = g * sig
            hidden = (act * u).astype(bf16)
            grad_up = (h * act).astype(bf16)
            grad_gate = (h * u * sig * (1.0 + g * (1.0 - sig))).astype(bf16)
            cat_ref[r, b : b + 128, 0:half] = grad_gate
            cat_ref[r, b : b + 128, half : 2 * half] = grad_up
            turn_ref[r, 0:half, b : b + 128] = grad_gate.T
            turn_ref[r, half : 2 * half, b : b + 128] = grad_up.T
            turn_ref[r, 2 * half : 3 * half, b : b + 128] = hidden.T


def forward(table, got, pairs, downs):
    half = pairs[0].shape[2]
    rows = COLS * ROWS
    return pl.pallas_call(
        forward_body,
        out_shape=[
            jax.ShapeDtypeStruct((2, rows, 2 * half), bf16),
            jax.ShapeDtypeStruct((2, 3 * half, rows), bf16),
        ],
        in_specs=[smem_spec()] + vmem_specs(33),
        out_specs=vmem_specs(2),
        scratch_shapes=[pltpu.VMEM((rows, 2 * half), f32), pltpu.VMEM((rows, half), f32)],
        compiler_params=params(),
        name="forward",
    )(table, got, *pairs, *downs)


def rows_body(table, cat_ref, *refs):
    pairs = refs[:16]
    out_ref, acc = refs[16:]
    width = acc.shape[2]
    for r in range(2):
        for k in range(r, RING, 2):
            for j in range(2):
                n = 2 * k + j
                part = dot(cat_ref[r], side_by_side(pairs[n]), contract_last)
                if r == 0:
                    acc[table[n]] = part
                else:
                    acc[table[n]] += part
    for d in range(acc.shape[0]):
        out_ref[:, d] = acc[d].astype(bf16).reshape(COLS, ROWS, width)


def row_grads(table, cat, pairs):
    width = pairs[0].shape[1]
    return pl.pallas_call(
        rows_body,
        out_shape=jax.ShapeDtypeStruct((COLS, RING, ROWS, width), bf16),
        in_specs=[smem_spec()] + vmem_specs(17),
        out_specs=pl.BlockSpec(memory_space=pltpu.VMEM),
        scratch_shapes=[pltpu.VMEM((RING, cat.shape[1], width), f32)],
        compiler_params=params(),
        name="row_grads",
    )(table, cat, *pairs)


def terms_body(table, turn_ref, tok_a, tok_b, cot_a, cot_b, own_ref, other_ref):
    half = turn_ref.shape[1] // 3
    for out, tok, cot in ((own_ref, tok_a, cot_a), (other_ref, tok_b, cot_b)):
        out[0, 0 : 2 * half, :] = dot(turn_ref[0, 0 : 2 * half, :], slice_of(tok, 0)).astype(bf16)
        out[0, 2 * half : 3 * half, :] = dot(
            turn_ref[0, 2 * half : 3 * half, :], slice_of(cot, 0)
        ).astype(bf16)


def weight_terms(table, turn, got, steps):
    _, triple, rows = turn.shape
    width = got.shape[3]
    at = [
        pl.BlockSpec((COLS, 1, ROWS, width), lambda g, t, j=j, n=n: (0, t[1 + j, g], n, 0))
        for n in range(2)
        for j in range(2)
    ]
    out = pl.BlockSpec((1, triple, width), lambda g, t: (g, 0, 0))
    shape = jax.ShapeDtypeStruct((len(steps), triple, width), bf16)
    own, other = pl.pallas_call(
        terms_body,
        out_shape=[shape, shape],
        grid_spec=pltpu.PrefetchScalarGridSpec(
            num_scalar_prefetch=1,
            grid=(len(steps),),
            in_specs=[pl.BlockSpec((1, triple, rows), lambda g, t: (t[0, g], 0, 0))] + at,
            out_specs=[out, out],
        ),
        compiler_params=params(),
        name="weight_terms",
    )(table, turn, got, got, got, got)
    return own, swap_core(other)


def adam_step(gradient, w_ref, m_ref, v_ref, w_out, m_out, v_out):
    weight = w_ref[0].astype(f32)
    first = beta_one * m_ref[0] + (1.0 - beta_one) * gradient
    second = beta_two * v_ref[0] + (1.0 - beta_two) * gradient * gradient
    update = (
        first / bias_one / (jnp.sqrt(second / bias_two) + epsilon) + decay_rate * weight
    )
    w_out[0] = (weight - learn_rate * update).astype(bf16)
    m_out[0] = first
    v_out[0] = second


def adam_body(turned, near, rise, fall, *refs):
    count = len(refs) // 6
    half = near.shape[0] // count
    for i in range(count):
        part = slice(i * half, (i + 1) * half)
        gradient = near[part, :] + rise[part, :].astype(f32) + fall[part, :].astype(f32)
        if turned:
            gradient = gradient.T
        ins = refs[3 * i : 3 * i + 3]
        outs = refs[3 * count + 3 * i : 3 * count + 3 * i + 3]
        adam_step(gradient, *ins, *outs)


def adam(turned, sums, *states):
    shapes = [
        jax.ShapeDtypeStruct(v.shape, bf16 if i % 3 == 0 else f32) for i, v in enumerate(states)
    ]
    return pl.pallas_call(
        functools.partial(adam_body, turned),
        out_shape=shapes,
        in_specs=vmem_specs(3 + len(states)),
        out_specs=vmem_specs(len(states)),
        compiler_params=params(),
        name="adam",
    )(*sums, *states)


def gather_ring(own, reaches):
    chunks = [[None] * RING for _ in own]
    rising, falling = list(own), list(own)
    for m, piece in enumerate(own):
        chunks[m][0] = piece
    for step in range(1, RING):
        for m, reach in enumerate(reaches):
            if step <= reach:
                rising[m] = up_z(rising[m])
                chunks[m][RING - step] = rising[m]
            if step <= RING - 1 - reach:
                falling[m] = down_z(falling[m])
                chunks[m][step] = falling[m]
    return [[v for c in chunk for v in (c, swap_core(c))] for chunk in chunks]


def ring_sum(mine, theirs, carried=None):
    total = mine.astype(f32) + theirs.astype(f32)
    return total if carried is None else total + carried.astype(f32)


def scatter_start(own, other, reach):
    fall = RING - 1 - reach
    return [ring_sum(own[k], other[k]).astype(bf16) for k in (reach, RING - fall)]


def first_hop(started):
    return [[up_z(v[0]), down_z(v[1])] for v in reversed(started)][::-1]


def scatter_rings(own, other, started, reaches):
    rising, falling = [v[0] for v in started], [v[1] for v in started]
    for step in range(1, RING):
        for m, reach in reversed(list(enumerate(reaches))):
            if step <= reach:
                rising[m] = up_z(rising[m]) if step > 1 else rising[m]
                if step < reach:
                    k = reach - step
                    rising[m] = ring_sum(own[m][k], other[m][k], rising[m]).astype(bf16)
            fall = RING - 1 - reach
            if step <= fall:
                falling[m] = down_z(falling[m]) if step > 1 else falling[m]
                if step < fall:
                    k = RING - fall + step
                    falling[m] = ring_sum(own[m][k], other[m][k], falling[m]).astype(bf16)
    near = [ring_sum(own[m][0], other[m][0]) for m in range(len(reaches))]
    return list(zip(near, rising, falling, strict=True))


def per_device(
    tokens,
    out_grad,
    expert_ids,
    gate_fixed,
    w_gate,
    w_up,
    w_down,
    m_gate,
    m_up,
    m_down,
    v_gate,
    v_up,
    v_down,
):
    zh, zl, core = lax.axis_index("zh"), lax.axis_index("zl"), lax.axis_index("c")
    rows = tokens.shape[0]
    half = w_gate.shape[2]

    def slices(steps):
        step = jnp.array(steps, jnp.int32)
        chip = (zh * 2 + zl + step) % RING
        return [step % 2] + [(chip // 2) * 2 + jnp.bitwise_xor(core, j) for j in range(2)]

    table = jnp.stack(slices(range(RING))[1:], axis=1).reshape(2 * RING).astype(jnp.int32)

    pick, sent = dispatch(
        expert_ids.reshape(1, rows), gate_fixed.reshape(1, rows), tokens, out_grad
    )
    (gate_own, up_own, down_own), sent = lax.optimization_barrier(((w_gate, w_up, w_down), sent))
    got = columns(sent)
    own_pair = jnp.concatenate([gate_own, up_own], axis=0)
    pairs, downs = gather_ring((own_pair, down_own[0]), REACH)
    cat, turn = forward(table, got, pairs, downs)

    cut = 2 * half
    own = [[None] * RING for _ in REACH]
    other = [[None] * RING for _ in REACH]

    def terms(turn, steps):
        at = jnp.stack(slices(steps)).astype(jnp.int32)
        mine, theirs = weight_terms(at, turn, got, steps)
        for i, k in enumerate(steps):
            own[0][k], own[1][k] = mine[i, :cut], mine[i, cut:]
            other[0][k], other[1][k] = theirs[i, :cut], theirs[i, cut:]
        return mine

    first = terms(turn, (4, 5, 3))
    cat, first = lax.optimization_barrier((cat, first))
    pieces = row_grads(table, cat, pairs)
    started = [scatter_start(own[m], other[m], REACH[m]) for m in range(len(REACH))]
    pieces, started = lax.optimization_barrier((pieces, started))
    back = columns(pieces)
    started = first_hop(started)
    turn, started[1][1] = lax.optimization_barrier((turn, started[1][1]))
    terms(turn, (6, 2, 7, 1, 0))
    input_grad = combine(pick, back)
    pair_sums, down_sums = scatter_rings(own, other, started, REACH)
    gate_up = adam(True, pair_sums, w_gate, m_gate, v_gate, w_up, m_up, v_up)
    down = adam(False, down_sums, w_down, m_down, v_down)
    return (input_grad,) + tuple(
        (gate_up[i], gate_up[3 + i], down[i])[m] for i in range(3) for m in range(3)
    )


def solution(mesh):
    fine = Mesh(mesh.devices.reshape(4, 2, SIDE, SIDE, 2), ("zh", "c", "y", "x", "zl"))
    rows = P(("zh", "c", "y", "x", "zl"), None)
    tall = P(("y", "x", "zl"), ("zh", "c"), None)
    wide = P(("y", "x", "zl"), None, ("zh", "c"))
    states = (tall, tall, wide)
    return jax.shard_map(
        per_device,
        mesh=fine,
        in_specs=(rows,) * 4 + states * 3,
        out_specs=(rows,) + states * 3,
        check_vma=False,
    )
```

```python
import functools

import jax
import jax.numpy as jnp
from jax import lax
from jax.experimental import pallas as pl
from jax.experimental.pallas import tpu as pltpu
from jax.sharding import Mesh
from jax.sharding import PartitionSpec as P


beta_one = 0.9
beta_two = 0.95
learn_rate = 0.002
decay_rate = 0.1
epsilon = 1e-08
bias_one = 1.0 - beta_one**20
bias_two = 1.0 - beta_two**20
fixed_scale = 1.0 / 65536.0

f32 = jnp.float32
bf16 = jnp.bfloat16
ROWS = 32
SIDE = 4
RING = 8
COLS = SIDE * SIDE
BLOCK = 256
PARTS = COLS * ROWS // BLOCK
REACH = (4, 3, 4)
VMEM_LIMIT = 56 * 1024 * 1024

contract_last = (((1,), (1,)), ((), ()))
contract_first = (((0,), (0,)), ((), ()))


def dot(a, b, dims=(((1,), (0,)), ((), ()))):
    return lax.dot_general(a, b, dims, preferred_element_type=f32)


def vmem_specs(n):
    return [pl.BlockSpec(memory_space=pltpu.VMEM)] * n


def smem_spec():
    return pl.BlockSpec(memory_space=pltpu.SMEM)


def params():
    return pltpu.CompilerParams(vmem_limit_bytes=VMEM_LIMIT)


def up_z(v):
    return lax.ppermute(v, ("zh", "zl"), [(i, (i + 1) % RING) for i in range(RING)])


def down_z(v):
    return lax.ppermute(v, ("zh", "zl"), [(i, (i - 1) % RING) for i in range(RING)])


def swap_core(v):
    return lax.ppermute(v, "c", [(0, 1), (1, 0)])


def columns(v):
    return lax.all_to_all(v, ("y", "x"), split_axis=0, concat_axis=0, tiled=True)


def dispatch_body(ids_ref, gate_ref, tok_ref, grad_ref, pick_ref, out_ref):
    rows = ids_ref.shape[1]
    ids = ids_ref[...]
    first = lax.broadcasted_iota(jnp.int32, (rows, rows), 0)
    second = lax.broadcasted_iota(jnp.int32, (rows, rows), 1)
    ones = jnp.where(ids == lax.broadcasted_iota(jnp.int32, (COLS, rows), 0), 1.0, 0.0)
    count = dot(ones.astype(bf16), jnp.where(first <= second, 1.0, 0.0).astype(bf16))
    position = jnp.sum(ones * count, axis=0, keepdims=True).astype(jnp.int32) - 1
    slot = ids * ROWS + position
    pick = jnp.where(
        lax.broadcasted_iota(jnp.int32, (COLS * ROWS, rows), 0) == slot, 1.0, 0.0
    ).astype(bf16)
    pick_ref[...] = pick
    scale_row = gate_ref[...].astype(f32) * fixed_scale
    scale = jnp.sum(jnp.where(first == second, scale_row, 0.0), axis=1, keepdims=True)
    tok = tok_ref[...]
    cot = (grad_ref[...].astype(f32) * scale).astype(bf16)
    width = out_ref.shape[3]
    for n, source in enumerate((tok, cot)):
        for d in range(RING):
            part = dot(pick, source[:, d * width : (d + 1) * width]).astype(bf16)
            out_ref[:, d, n * ROWS : (n + 1) * ROWS, :] = part.reshape(COLS, ROWS, width)


def dispatch(ids, gate, tokens, out_grad):
    rows, width = tokens.shape
    return pl.pallas_call(
        dispatch_body,
        out_shape=[
            jax.ShapeDtypeStruct((COLS * ROWS, rows), bf16),
            jax.ShapeDtypeStruct((COLS, RING, 2 * ROWS, width // RING), bf16),
        ],
        in_specs=vmem_specs(4),
        out_specs=vmem_specs(2),
        compiler_params=params(),
        name="dispatch",
    )(ids, gate, tokens, out_grad)


def combine_body(pick_ref, back_ref, out_ref):
    width = back_ref.shape[3]
    for d in range(RING):
        rows = back_ref[:, d].reshape(COLS * ROWS, width)
        part = dot(pick_ref[...], rows, contract_first)
        out_ref[:, d * width : (d + 1) * width] = part.astype(bf16)


def combine(pick, back):
    return pl.pallas_call(
        combine_body,
        out_shape=jax.ShapeDtypeStruct((pick.shape[1], RING * back.shape[3]), bf16),
        in_specs=vmem_specs(2),
        out_specs=pl.BlockSpec(memory_space=pltpu.VMEM),
        compiler_params=params(),
        name="combine",
    )(pick, back)


def block_of(got, b, d, n):
    per = BLOCK // ROWS
    rows = got[pl.ds(b * per, per), d, n * ROWS : (n + 1) * ROWS, :]
    return rows.reshape(BLOCK, got.shape[3])


def forward_body(table, got, *refs):
    gates = refs[:16]
    ups = refs[16:32]
    downs = refs[32:48]
    cat_ref, turn_ref, pre_acc, cot_acc = refs[48:]
    half = cot_acc.shape[1]

    def block(b, carry):
        for r in range(2):
            for k in range(r, RING, 2):
                for n in (2 * k, 2 * k + 1):
                    tok = block_of(got, b, table[n], 0)
                    cot = block_of(got, b, table[n], 1)
                    wide = jnp.concatenate([gates[n][...], ups[n][...]], axis=1)
                    pre = dot(tok, wide)
                    hid = dot(cot, downs[n][...], contract_last)
                    if n == 2 * r:
                        pre_acc[...] = pre
                        cot_acc[...] = hid
                    else:
                        pre_acc[...] += pre
                        cot_acc[...] += hid
            g = pre_acc[:, 0:half]
            u = pre_acc[:, half : 2 * half]
            h = cot_acc[...]
            sig = jax.nn.sigmoid(g)
            act = g * sig
            hidden = (act * u).astype(bf16)
            grad_up = (h * act).astype(bf16)
            grad_gate = (h * u * sig * (1.0 + g * (1.0 - sig))).astype(bf16)
            cat_ref[r, b, :, 0:half] = grad_gate
            cat_ref[r, b, :, half : 2 * half] = grad_up
            turn_ref[r, b, 0:half, :] = grad_gate.T
            turn_ref[r, b, half : 2 * half, :] = grad_up.T
            turn_ref[r, b, 2 * half : 3 * half, :] = hidden.T
        return carry

    lax.fori_loop(0, PARTS, block, 0)


def forward(table, got, gates, ups, downs):
    half = gates[0].shape[1]
    return pl.pallas_call(
        forward_body,
        out_shape=[
            jax.ShapeDtypeStruct((2, PARTS, BLOCK, 2 * half), bf16),
            jax.ShapeDtypeStruct((2, PARTS, 3 * half, BLOCK), bf16),
        ],
        in_specs=[smem_spec()] + vmem_specs(49),
        out_specs=vmem_specs(2),
        scratch_shapes=[pltpu.VMEM((BLOCK, 2 * half), f32), pltpu.VMEM((BLOCK, half), f32)],
        compiler_params=params(),
        name="forward",
    )(table, got, *gates, *ups, *downs)


def rows_body(table, cat_ref, *refs):
    gates = refs[:16]
    ups = refs[16:32]
    out_ref, acc = refs[32:]
    width = acc.shape[2]
    per = BLOCK // ROWS

    def block(b, carry):
        for r in range(2):
            for n in (n for k in range(r, RING, 2) for n in (2 * k, 2 * k + 1)):
                wide = jnp.concatenate([gates[n][...], ups[n][...]], axis=1)
                part = dot(cat_ref[r, b], wide, contract_last)
                if r == 0:
                    acc[table[n]] = part
                else:
                    total = (acc[table[n]] + part).astype(bf16)
                    out_ref[pl.ds(b * per, per), table[n]] = total.reshape(per, ROWS, width)
        return carry

    lax.fori_loop(0, PARTS, block, 0)


def row_grads(table, cat, gates, ups):
    width = gates[0].shape[0]
    return pl.pallas_call(
        rows_body,
        out_shape=jax.ShapeDtypeStruct((COLS, RING, ROWS, width), bf16),
        in_specs=[smem_spec()] + vmem_specs(33),
        out_specs=pl.BlockSpec(memory_space=pltpu.VMEM),
        scratch_shapes=[pltpu.VMEM((RING, BLOCK, width), f32)],
        compiler_params=params(),
        name="row_grads",
    )(table, cat, *gates, *ups)


def terms_body(table, turn_ref, near_ref, far_ref, own_ref, other_ref):
    half = turn_ref.shape[2] // 3
    per = BLOCK // ROWS

    def third(i, carry):
        at = lax.div(i, 2) * ROWS
        rows = pl.ds(pl.multiple_of(i * half, half), half)
        for out, ref in ((own_ref, near_ref), (other_ref, far_ref)):
            total = None
            for b in range(PARTS):
                right = ref[b * per : (b + 1) * per, 0, pl.ds(pl.multiple_of(at, ROWS), ROWS), :]
                part = dot(turn_ref[0, b, rows, :], right.reshape(BLOCK, ref.shape[3]))
                total = part if total is None else total + part
            out[0, rows, :] = total.astype(bf16)
        return carry

    lax.fori_loop(0, 3, third, 0)


def weight_terms(table, turn, got, steps):
    _, parts, triple, rows = turn.shape
    width = got.shape[3]
    at = [
        pl.BlockSpec((COLS, 1, 2 * ROWS, width), lambda g, t, j=j: (0, t[1 + j, g], 0, 0))
        for j in range(2)
    ]
    out = pl.BlockSpec((1, triple, width), lambda g, t: (g, 0, 0))
    shape = jax.ShapeDtypeStruct((len(steps), triple, width), bf16)
    own, other = pl.pallas_call(
        terms_body,
        out_shape=[shape, shape],
        grid_spec=pltpu.PrefetchScalarGridSpec(
            num_scalar_prefetch=1,
            grid=(len(steps),),
            in_specs=[pl.BlockSpec((1, parts, triple, rows), lambda g, t: (t[0, g], 0, 0, 0))] + at,
            out_specs=[out, out],
        ),
        compiler_params=params(),
        name="weight_terms",
    )(table, turn, got, got)
    return own, swap_core(other)


def adam_step(gradient, w_ref, m_ref, v_ref, w_out, m_out, v_out):
    weight = w_ref[0].astype(f32)
    first = beta_one * m_ref[0] + (1.0 - beta_one) * gradient
    second = beta_two * v_ref[0] + (1.0 - beta_two) * gradient * gradient
    update = (
        first / bias_one / (jnp.sqrt(second / bias_two) + epsilon) + decay_rate * weight
    )
    w_out[0] = (weight - learn_rate * update).astype(bf16)
    m_out[0] = first
    v_out[0] = second


def adam_body(turned, near, rise, fall, *refs):
    gradient = near[...] + rise[...].astype(f32) + fall[...].astype(f32)
    adam_step(gradient.T if turned else gradient, *refs)


def adam(turned, sums, *state):
    return pl.pallas_call(
        functools.partial(adam_body, turned),
        out_shape=[jax.ShapeDtypeStruct(v.shape, v.dtype) for v in state],
        in_specs=vmem_specs(6),
        out_specs=vmem_specs(3),
        compiler_params=params(),
        name="adam",
    )(*sums, *state)


def gather_ring(own, reaches):
    chunks = [[None] * RING for _ in own]
    rising, falling = list(own), list(own)
    for m, piece in enumerate(own):
        chunks[m][0] = piece
    for step in range(1, RING):
        for m, reach in enumerate(reaches):
            if step <= reach:
                rising[m] = up_z(rising[m])
                chunks[m][RING - step] = rising[m]
            if step <= RING - 1 - reach:
                falling[m] = down_z(falling[m])
                chunks[m][step] = falling[m]
    return [[v for c in chunk for v in (c, swap_core(c))] for chunk in chunks]


def ring_sum(mine, theirs, carried=None):
    (own, at, part), other = mine, theirs[0]
    if carried is None:
        return own[at, part].astype(f32) + other[at, part].astype(f32)
    own, other, carried = lax.optimization_barrier((own, other, carried))
    return own[at, part].astype(f32) + other[at, part].astype(f32) + carried.astype(f32)


def scatter_start(own, other, reach):
    fall = RING - 1 - reach
    return [ring_sum(own[k], other[k]).astype(bf16) for k in (reach, RING - fall)]


def later_hops(own, other, rising, falling, reaches):
    count = range(len(reaches))
    for step in range(1, RING):
        for m in count:
            if 1 < step <= reaches[m]:
                k = reaches[m] - step + 1
                rising[m] = up_z(ring_sum(own[m][k], other[m][k], rising[m]).astype(bf16))
        for m in count:
            fall = RING - 1 - reaches[m]
            if 1 < step <= fall:
                k = RING - fall + step - 1
                falling[m] = down_z(ring_sum(own[m][k], other[m][k], falling[m]).astype(bf16))
    near = [ring_sum(own[m][0], other[m][0]) for m in count]
    return list(zip(near, rising, falling, strict=True))


def per_device(
    tokens,
    out_grad,
    expert_ids,
    gate_fixed,
    w_gate,
    w_up,
    w_down,
    m_gate,
    m_up,
    m_down,
    v_gate,
    v_up,
    v_down,
):
    zh, zl, core = lax.axis_index("zh"), lax.axis_index("zl"), lax.axis_index("c")
    rows = tokens.shape[0]
    half = w_gate.shape[2]

    def slices(steps):
        step = jnp.array(steps, jnp.int32)
        chip = (zh * 2 + zl + step) % RING
        return [step % 2] + [(chip // 2) * 2 + jnp.bitwise_xor(core, j) for j in range(2)]

    table = jnp.stack(slices(range(RING))[1:], axis=1).reshape(2 * RING).astype(jnp.int32)

    pick, sent = dispatch(
        expert_ids.reshape(1, rows), gate_fixed.reshape(1, rows), tokens, out_grad
    )
    (gate_own, up_own, down_own), sent = lax.optimization_barrier(((w_gate, w_up, w_down), sent))
    got = columns(sent)
    weights = (gate_own[0], up_own[0], down_own[0])
    gates, ups, downs = gather_ring(weights, REACH)
    cat, turn = forward(table, got, gates, ups, downs)

    own = [[None] * RING for _ in REACH]
    other = [[None] * RING for _ in REACH]

    def terms(turn, steps):
        at = jnp.stack(slices(steps)).astype(jnp.int32)
        mine, theirs = weight_terms(at, turn, got, steps)
        for i, k in enumerate(steps):
            for m in range(3):
                part = slice(m * half, (m + 1) * half)
                own[m][k], other[m][k] = (mine, i, part), (theirs, i, part)
        return mine

    first = terms(turn, (4, 5, 3))
    cat, first = lax.optimization_barrier((cat, first))
    pieces = row_grads(table, cat, gates, ups)
    started = [scatter_start(own[m], other[m], REACH[m]) for m in range(3)]
    pieces, started = lax.optimization_barrier((pieces, started))
    rising = [up_z(v[0]) for v in started]
    falling = [down_z(v[1]) for v in started]
    back = columns(pieces)
    turn, pieces = lax.optimization_barrier((turn, pieces))
    second = terms(turn, (6, 2))
    turn, second = lax.optimization_barrier((turn, second))
    terms(turn, (7, 1, 0))
    sums = later_hops(own, other, rising, falling, REACH)
    input_grad = combine(pick, back)
    gate = adam(True, sums[0], w_gate, m_gate, v_gate)
    up = adam(True, sums[1], w_up, m_up, v_up)
    down = adam(False, sums[2], w_down, m_down, v_down)
    return (input_grad,) + tuple(v[i] for i in range(3) for v in (gate, up, down))


def solution(mesh):
    fine = Mesh(mesh.devices.reshape(4, 2, SIDE, SIDE, 2), ("zh", "c", "y", "x", "zl"))
    rows = P(("zh", "c", "y", "x", "zl"), None)
    tall = P(("y", "x", "zl"), ("zh", "c"), None)
    wide = P(("y", "x", "zl"), None, ("zh", "c"))
    states = (tall, tall, wide)
    return jax.shard_map(
        per_device,
        mesh=fine,
        in_specs=(rows,) * 4 + states * 3,
        out_specs=(rows,) + states * 3,
        check_vma=False,
    )
```

```python
import functools

import jax
import jax.numpy as jnp
from jax import lax
from jax.experimental import pallas as pl
from jax.experimental.pallas import tpu as pltpu
from jax.sharding import Mesh
from jax.sharding import PartitionSpec as P


beta_one = 0.9
beta_two = 0.95
learn_rate = 0.002
decay_rate = 0.1
epsilon = 1e-08
bias_one = 1.0 - beta_one**20
bias_two = 1.0 - beta_two**20
fixed_scale = 1.0 / 65536.0

f32 = jnp.float32
bf16 = jnp.bfloat16
ROWS = 32
SIDE = 4
RING = 8
COLS = SIDE * SIDE
BLOCK = 256
PARTS = COLS * ROWS // BLOCK
REACH = (4, 3)
GROUPS = ((0, 7, 1, 6, 2), (5, 3, 4))
STEPS = tuple(k for group in GROUPS for k in group)
VMEM_LIMIT = 56 * 1024 * 1024

contract_last = (((1,), (1,)), ((), ()))
contract_first = (((0,), (0,)), ((), ()))


def dot(a, b, dims=(((1,), (0,)), ((), ()))):
    return lax.dot_general(a, b, dims, preferred_element_type=f32)


def vmem_specs(n):
    return [pl.BlockSpec(memory_space=pltpu.VMEM)] * n


def smem_spec():
    return pl.BlockSpec(memory_space=pltpu.SMEM)


def params():
    return pltpu.CompilerParams(vmem_limit_bytes=VMEM_LIMIT)


def up_z(v):
    return lax.ppermute(v, ("zh", "zl"), [(i, (i + 1) % RING) for i in range(RING)])


def down_z(v):
    return lax.ppermute(v, ("zh", "zl"), [(i, (i - 1) % RING) for i in range(RING)])


def swap_core(v):
    return lax.ppermute(v, "c", [(0, 1), (1, 0)])


def columns(v):
    return lax.all_to_all(v, ("y", "x"), split_axis=0, concat_axis=0, tiled=True)


def dispatch_body(ids_ref, gate_ref, tok_ref, grad_ref, pick_ref, out_ref):
    rows = ids_ref.shape[1]
    ids = ids_ref[...]
    first = lax.broadcasted_iota(jnp.int32, (rows, rows), 0)
    second = lax.broadcasted_iota(jnp.int32, (rows, rows), 1)
    ones = jnp.where(ids == lax.broadcasted_iota(jnp.int32, (COLS, rows), 0), 1.0, 0.0)
    count = dot(ones.astype(bf16), jnp.where(first <= second, 1.0, 0.0).astype(bf16))
    position = jnp.sum(ones * count, axis=0, keepdims=True).astype(jnp.int32) - 1
    slot = ids * ROWS + position
    pick = jnp.where(
        lax.broadcasted_iota(jnp.int32, (COLS * ROWS, rows), 0) == slot, 1.0, 0.0
    ).astype(bf16)
    pick_ref[...] = pick
    scale_row = gate_ref[...].astype(f32) * fixed_scale
    scale = jnp.sum(jnp.where(first == second, scale_row, 0.0), axis=1, keepdims=True)
    tok = tok_ref[...]
    cot = (grad_ref[...].astype(f32) * scale).astype(bf16)
    width = out_ref.shape[3]
    for n, source in enumerate((tok, cot)):
        for d in range(RING):
            part = dot(pick, source[:, d * width : (d + 1) * width]).astype(bf16)
            out_ref[:, d, n * ROWS : (n + 1) * ROWS, :] = part.reshape(COLS, ROWS, width)


def dispatch(ids, gate, tokens, out_grad):
    rows, width = tokens.shape
    return pl.pallas_call(
        dispatch_body,
        out_shape=[
            jax.ShapeDtypeStruct((COLS * ROWS, rows), bf16),
            jax.ShapeDtypeStruct((COLS, RING, 2 * ROWS, width // RING), bf16),
        ],
        in_specs=vmem_specs(4),
        out_specs=vmem_specs(2),
        compiler_params=params(),
        name="dispatch",
    )(ids, gate, tokens, out_grad)


def combine_body(pick_ref, back_ref, out_ref):
    width = back_ref.shape[3]
    for d in range(RING):
        rows = back_ref[:, d].reshape(COLS * ROWS, width)
        part = dot(pick_ref[...], rows, contract_first)
        out_ref[:, d * width : (d + 1) * width] = part.astype(bf16)


def combine(pick, back):
    return pl.pallas_call(
        combine_body,
        out_shape=jax.ShapeDtypeStruct((pick.shape[1], RING * back.shape[3]), bf16),
        in_specs=vmem_specs(2),
        out_specs=pl.BlockSpec(memory_space=pltpu.VMEM),
        compiler_params=params(),
        name="combine",
    )(pick, back)


def block_of(got, b, d, n):
    per = BLOCK // ROWS
    rows = got[pl.ds(b * per, per), d, n * ROWS : (n + 1) * ROWS, :]
    return rows.reshape(BLOCK, got.shape[3])


def place_of(refs, n):
    k, core = n // 2, n % 2
    group = next(g for g, steps in enumerate(GROUPS) if k in steps)
    return refs[2 * group + core], GROUPS[group].index(k)


def pair_of(refs, n):
    ref, i = place_of(refs, n)
    return jnp.concatenate([ref[i, 0], ref[i, 1]], axis=1)


def forward_body(table, got, *refs):
    pairs, downs = refs[:4], refs[4:8]
    cat_ref, turn_ref, pre_acc, cot_acc = refs[8:]
    half = cot_acc.shape[1]

    def block(b, carry):
        for r in range(2):
            for k in range(r, RING, 2):
                for n in (2 * k, 2 * k + 1):
                    tok = block_of(got, b, table[n], 0)
                    cot = block_of(got, b, table[n], 1)
                    pre = dot(tok, pair_of(pairs, n))
                    ref, i = place_of(downs, n)
                    hid = dot(cot, ref[i], contract_last)
                    if n == 2 * r:
                        pre_acc[...] = pre
                        cot_acc[...] = hid
                    else:
                        pre_acc[...] += pre
                        cot_acc[...] += hid
            g = pre_acc[:, 0:half]
            u = pre_acc[:, half : 2 * half]
            h = cot_acc[...]
            sig = jax.nn.sigmoid(g)
            act = g * sig
            hidden = (act * u).astype(bf16)
            grad_up = (h * act).astype(bf16)
            grad_gate = (h * u * sig * (1.0 + g * (1.0 - sig))).astype(bf16)
            cat_ref[r, b, :, 0:half] = grad_gate
            cat_ref[r, b, :, half : 2 * half] = grad_up
            turn_ref[r, b, 0:half, :] = grad_gate.T
            turn_ref[r, b, half : 2 * half, :] = grad_up.T
            turn_ref[r, b, 2 * half : 3 * half, :] = hidden.T
        return carry

    lax.fori_loop(0, PARTS, block, 0)


def forward(table, got, pairs, downs):
    half = pairs[0].shape[3]
    return pl.pallas_call(
        forward_body,
        out_shape=[
            jax.ShapeDtypeStruct((2, PARTS, BLOCK, 2 * half), bf16),
            jax.ShapeDtypeStruct((2, PARTS, 3 * half, BLOCK), bf16),
        ],
        in_specs=[smem_spec()] + vmem_specs(9),
        out_specs=vmem_specs(2),
        scratch_shapes=[pltpu.VMEM((BLOCK, 2 * half), f32), pltpu.VMEM((BLOCK, half), f32)],
        compiler_params=params(),
        name="forward",
    )(table, got, *pairs, *downs)


def rows_body(table, cat_ref, *refs):
    pairs = refs[:4]
    out_ref, acc = refs[4:]
    width = acc.shape[2]
    per = BLOCK // ROWS

    def block(b, carry):
        for r in range(2):
            for n in (n for k in range(r, RING, 2) for n in (2 * k, 2 * k + 1)):
                part = dot(cat_ref[r, b], pair_of(pairs, n), contract_last)
                if r == 0:
                    acc[table[n]] = part
                else:
                    total = (acc[table[n]] + part).astype(bf16)
                    out_ref[pl.ds(b * per, per), table[n]] = total.reshape(per, ROWS, width)
        return carry

    lax.fori_loop(0, PARTS, block, 0)


def row_grads(table, cat, pairs):
    width = pairs[0].shape[2]
    return pl.pallas_call(
        rows_body,
        out_shape=jax.ShapeDtypeStruct((COLS, RING, ROWS, width), bf16),
        in_specs=[smem_spec()] + vmem_specs(5),
        out_specs=pl.BlockSpec(memory_space=pltpu.VMEM),
        scratch_shapes=[pltpu.VMEM((RING, BLOCK, width), f32)],
        compiler_params=params(),
        name="row_grads",
    )(table, cat, *pairs)


def terms_body(table, turn_ref, near_ref, far_ref, own_ref, other_ref):
    half = turn_ref.shape[2] // 3
    per = BLOCK // ROWS
    for out, ref in ((own_ref, near_ref), (other_ref, far_ref)):
        for n, part in enumerate((slice(0, 2 * half), slice(2 * half, 3 * half))):
            total = None
            for b in range(PARTS):
                right = ref[b * per : (b + 1) * per, 0, n * ROWS : (n + 1) * ROWS, :]
                product = dot(turn_ref[0, b, part, :], right.reshape(BLOCK, ref.shape[3]))
                total = product if total is None else total + product
            out[0, part, :] = total.astype(bf16)


def weight_terms(table, turn, got, steps):
    _, parts, triple, rows = turn.shape
    width = got.shape[3]
    at = [
        pl.BlockSpec((COLS, 1, 2 * ROWS, width), lambda g, t, j=j: (0, t[1 + j, g], 0, 0))
        for j in range(2)
    ]
    out = pl.BlockSpec((1, triple, width), lambda g, t: (g, 0, 0))
    shape = jax.ShapeDtypeStruct((len(steps), triple, width), bf16)
    own, other = pl.pallas_call(
        terms_body,
        out_shape=[shape, shape],
        grid_spec=pltpu.PrefetchScalarGridSpec(
            num_scalar_prefetch=1,
            grid=(len(steps),),
            in_specs=[pl.BlockSpec((1, parts, triple, rows), lambda g, t: (t[0, g], 0, 0, 0))] + at,
            out_specs=[out, out],
        ),
        compiler_params=params(),
        name="weight_terms",
    )(table, turn, got, got)
    return own, other


def adam_step(gradient, w_ref, m_ref, v_ref, w_out, m_out, v_out):
    weight = w_ref[0].astype(f32)
    first = beta_one * m_ref[0] + (1.0 - beta_one) * gradient
    second = beta_two * v_ref[0] + (1.0 - beta_two) * gradient * gradient
    update = (
        first / bias_one / (jnp.sqrt(second / bias_two) + epsilon) + decay_rate * weight
    )
    w_out[0] = (weight - learn_rate * update).astype(bf16)
    m_out[0] = first
    v_out[0] = second


def adam_body(turned, own_ref, other_ref, rise, fall, *refs):
    gradient = own_ref[0].astype(f32) + other_ref[0].astype(f32)
    gradient = gradient + rise[...].astype(f32) + fall[...].astype(f32)
    adam_step(gradient.T if turned else gradient, *refs)


def adam(turned, own, other, m, rise, fall, row, *state):
    half, width = own.shape[1] // 3, own.shape[2]
    near = pl.BlockSpec((1, half, width), lambda g: (STEPS.index(0), m, 0))
    sums = pl.BlockSpec((half, width), lambda g: (row, 0))
    whole = [pl.BlockSpec(v.shape, lambda g: (0, 0, 0)) for v in state]
    return pl.pallas_call(
        functools.partial(adam_body, turned),
        grid=(1,),
        out_shape=[jax.ShapeDtypeStruct(v.shape, v.dtype) for v in state],
        in_specs=[near, near, sums, sums] + whole,
        out_specs=whole,
        compiler_params=params(),
        name="adam",
    )(own, other, rise, fall, *state)


def gather_ring(own, reaches):
    chunks = [[None] * RING for _ in own]
    rising, falling = list(own), list(own)
    for m, piece in enumerate(own):
        chunks[m][0] = piece
    for step in range(1, RING):
        for m, reach in enumerate(reaches):
            if step <= reach:
                rising[m] = up_z(rising[m])
                chunks[m][RING - step] = rising[m]
            if step <= RING - 1 - reach:
                falling[m] = down_z(falling[m])
                chunks[m][step] = falling[m]
    groups = [[jnp.stack([chunk[k] for k in steps]) for steps in GROUPS] for chunk in chunks]
    return [[v for group in piece for v in (group, swap_core(group))] for piece in groups]


def ring_sum(own, other, k, part, carried=None):
    at = STEPS.index(k)
    if carried is None:
        return (own[at, part].astype(f32) + other[at, part].astype(f32)).astype(bf16)
    own, other, carried = lax.optimization_barrier((own, other, carried))
    total = own[at, part].astype(f32) + other[at, part].astype(f32) + carried.astype(f32)
    return total.astype(bf16)


def scatter_ring(own, other, parts, reaches):
    rising = [ring_sum(own, other, reach, part) for part, reach in zip(parts, reaches)]
    falling = [ring_sum(own, other, reach + 1, part) for part, reach in zip(parts, reaches)]
    for step in range(1, RING):
        for m, reach in reversed(list(enumerate(reaches))):
            if step <= reach:
                if step > 1:
                    k = reach - step + 1
                    rising[m] = ring_sum(own, other, k, parts[m], rising[m])
                rising[m] = up_z(rising[m])
            if step <= RING - 1 - reach:
                if step > 1:
                    k = reach + step
                    falling[m] = ring_sum(own, other, k, parts[m], falling[m])
                falling[m] = down_z(falling[m])
    return list(zip(rising, falling, strict=True))


def per_device(
    tokens,
    out_grad,
    expert_ids,
    gate_fixed,
    w_gate,
    w_up,
    w_down,
    m_gate,
    m_up,
    m_down,
    v_gate,
    v_up,
    v_down,
):
    zh, zl, core = lax.axis_index("zh"), lax.axis_index("zl"), lax.axis_index("c")
    rows = tokens.shape[0]
    half = w_gate.shape[2]

    def slices(steps):
        step = jnp.array(steps, jnp.int32)
        chip = (zh * 2 + zl + step) % RING
        return [step % 2] + [(chip // 2) * 2 + jnp.bitwise_xor(core, j) for j in range(2)]

    table = jnp.stack(slices(range(RING))[1:], axis=1).reshape(2 * RING).astype(jnp.int32)

    pick, sent = dispatch(
        expert_ids.reshape(1, rows), gate_fixed.reshape(1, rows), tokens, out_grad
    )
    (gate_own, up_own, down_own), sent = lax.optimization_barrier(((w_gate, w_up, w_down), sent))
    got = columns(sent)
    weights = (jnp.concatenate([gate_own, up_own], axis=0), down_own[0])
    pairs, downs = gather_ring(weights, REACH)
    cat, turn = forward(table, got, pairs, downs)

    at = jnp.stack(slices(STEPS)).astype(jnp.int32)
    own, other = weight_terms(at, turn, got, STEPS)
    cat, own, other = lax.optimization_barrier((cat, own, other))
    other = swap_core(other)
    pieces = row_grads(table, cat, pairs)
    back = columns(pieces)
    parts = (slice(0, 2 * half), slice(2 * half, 3 * half))
    sums = scatter_ring(own, other, parts, REACH)
    input_grad = combine(pick, back)
    gate = adam(True, own, other, 0, *sums[0], 0, w_gate, m_gate, v_gate)
    up = adam(True, own, other, 1, *sums[0], 1, w_up, m_up, v_up)
    down = adam(False, own, other, 2, *sums[1], 0, w_down, m_down, v_down)
    return (input_grad,) + tuple(v[i] for i in range(3) for v in (gate, up, down))


def solution(mesh):
    fine = Mesh(mesh.devices.reshape(4, 2, SIDE, SIDE, 2), ("zh", "c", "y", "x", "zl"))
    rows = P(("zh", "c", "y", "x", "zl"), None)
    tall = P(("y", "x", "zl"), ("zh", "c"), None)
    wide = P(("y", "x", "zl"), None, ("zh", "c"))
    states = (tall, tall, wide)
    return jax.shard_map(
        per_device,
        mesh=fine,
        in_specs=(rows,) * 4 + states * 3,
        out_specs=(rows,) + states * 3,
        check_vma=False,
    )
```

```python
import jax
import jax.numpy as jnp
from jax import lax
from jax.experimental import pallas as pl
from jax.experimental.pallas import tpu as pltpu
from jax.sharding import Mesh
from jax.sharding import PartitionSpec as P


beta_one = 0.9
beta_two = 0.95
learn_rate = 0.002
decay_rate = 0.1
epsilon = 1e-08
bias_one = 1.0 - beta_one**20
bias_two = 1.0 - beta_two**20
fixed_scale = 1.0 / 65536.0

f32 = jnp.float32
bf16 = jnp.bfloat16
ROWS = 32
SIDE = 4
RING = 8
COLS = SIDE * SIDE
BLOCK = 256
PARTS = COLS * ROWS // BLOCK
REACH = (4, 3)
GROUPS = ((0, 7, 1, 6, 2), (5, 3, 4))
TERMS = (0, 2, 4, 6, 1, 3, 5, 7)
VMEM_LIMIT = 56 * 1024 * 1024

contract_last = (((1,), (1,)), ((), ()))
contract_first = (((0,), (0,)), ((), ()))


def dot(a, b, dims=(((1,), (0,)), ((), ()))):
    return lax.dot_general(a, b, dims, preferred_element_type=f32)


def vmem_specs(n):
    return [pl.BlockSpec(memory_space=pltpu.VMEM)] * n


def smem_spec():
    return pl.BlockSpec(memory_space=pltpu.SMEM)


def params():
    return pltpu.CompilerParams(vmem_limit_bytes=VMEM_LIMIT)


def up_z(v):
    return lax.ppermute(v, ("zh", "zl"), [(i, (i + 1) % RING) for i in range(RING)])


def down_z(v):
    return lax.ppermute(v, ("zh", "zl"), [(i, (i - 1) % RING) for i in range(RING)])


def swap_core(v):
    return lax.ppermute(v, "c", [(0, 1), (1, 0)])


def columns(v):
    return lax.all_to_all(v, ("y", "x"), split_axis=0, concat_axis=0, tiled=True)


def dispatch_body(ids_ref, gate_ref, tok_ref, grad_ref, pick_ref, out_ref):
    rows = ids_ref.shape[1]
    ids = ids_ref[...]
    first = lax.broadcasted_iota(jnp.int32, (rows, rows), 0)
    second = lax.broadcasted_iota(jnp.int32, (rows, rows), 1)
    ones = jnp.where(ids == lax.broadcasted_iota(jnp.int32, (COLS, rows), 0), 1.0, 0.0)
    count = dot(ones.astype(bf16), jnp.where(first <= second, 1.0, 0.0).astype(bf16))
    position = jnp.sum(ones * count, axis=0, keepdims=True).astype(jnp.int32) - 1
    slot = ids * ROWS + position
    pick = jnp.where(
        lax.broadcasted_iota(jnp.int32, (COLS * ROWS, rows), 0) == slot, 1.0, 0.0
    ).astype(bf16)
    pick_ref[...] = pick
    scale_row = gate_ref[...].astype(f32) * fixed_scale
    scale = jnp.sum(jnp.where(first == second, scale_row, 0.0), axis=1, keepdims=True)
    tok = tok_ref[...]
    cot = (grad_ref[...].astype(f32) * scale).astype(bf16)
    width = out_ref.shape[3]
    for n, source in enumerate((tok, cot)):
        for d in range(RING):
            part = dot(pick, source[:, d * width : (d + 1) * width]).astype(bf16)
            out_ref[:, d, n * ROWS : (n + 1) * ROWS, :] = part.reshape(COLS, ROWS, width)


def dispatch(ids, gate, tokens, out_grad):
    rows, width = tokens.shape
    return pl.pallas_call(
        dispatch_body,
        out_shape=[
            jax.ShapeDtypeStruct((COLS * ROWS, rows), bf16),
            jax.ShapeDtypeStruct((COLS, RING, 2 * ROWS, width // RING), bf16),
        ],
        in_specs=vmem_specs(4),
        out_specs=vmem_specs(2),
        compiler_params=params(),
        name="dispatch",
    )(ids, gate, tokens, out_grad)


def combine_body(pick_ref, back_ref, out_ref):
    width = back_ref.shape[3]
    for d in range(RING):
        rows = back_ref[:, d].reshape(COLS * ROWS, width)
        part = dot(pick_ref[...], rows, contract_first)
        out_ref[:, d * width : (d + 1) * width] = part.astype(bf16)


def combine(pick, back):
    return pl.pallas_call(
        combine_body,
        out_shape=jax.ShapeDtypeStruct((pick.shape[1], RING * back.shape[3]), bf16),
        in_specs=vmem_specs(2),
        out_specs=pl.BlockSpec(memory_space=pltpu.VMEM),
        compiler_params=params(),
        name="combine",
    )(pick, back)


def block_of(got, b, d, n):
    per = BLOCK // ROWS
    rows = got[pl.ds(b * per, per), d, n * ROWS : (n + 1) * ROWS, :]
    return rows.reshape(BLOCK, got.shape[3])


def place_of(refs, n):
    k, core = n // 2, n % 2
    group = next(g for g, steps in enumerate(GROUPS) if k in steps)
    return refs[2 * group + core], GROUPS[group].index(k)


def pair_of(refs, n):
    ref, i = place_of(refs, n)
    return jnp.concatenate([ref[i, 0], ref[i, 1]], axis=1)


def forward_body(table, got, *refs):
    pairs, downs = refs[:4], refs[4:8]
    cat_ref, turn_ref, pre_acc, cot_acc = refs[8:]
    half = cot_acc.shape[1]

    def block(b, carry):
        for r in range(2):
            for k in range(r, RING, 2):
                for n in (2 * k, 2 * k + 1):
                    tok = block_of(got, b, table[n], 0)
                    cot = block_of(got, b, table[n], 1)
                    pre = dot(tok, pair_of(pairs, n))
                    ref, i = place_of(downs, n)
                    hid = dot(cot, ref[i], contract_last)
                    if n == 2 * r:
                        pre_acc[...] = pre
                        cot_acc[...] = hid
                    else:
                        pre_acc[...] += pre
                        cot_acc[...] += hid
            g = pre_acc[:, 0:half]
            u = pre_acc[:, half : 2 * half]
            h = cot_acc[...]
            sig = jax.nn.sigmoid(g)
            act = g * sig
            hidden = (act * u).astype(bf16)
            grad_up = (h * act).astype(bf16)
            grad_gate = (h * u * sig * (1.0 + g * (1.0 - sig))).astype(bf16)
            cat_ref[r, b, :, 0:half] = grad_gate
            cat_ref[r, b, :, half : 2 * half] = grad_up
            turn_ref[r, b, 0:half, :] = grad_gate.T
            turn_ref[r, b, half : 2 * half, :] = grad_up.T
            turn_ref[r, b, 2 * half : 3 * half, :] = hidden.T
        return carry

    lax.fori_loop(0, PARTS, block, 0)


def forward(table, got, pairs, downs):
    half = pairs[0].shape[3]
    return pl.pallas_call(
        forward_body,
        out_shape=[
            jax.ShapeDtypeStruct((2, PARTS, BLOCK, 2 * half), bf16),
            jax.ShapeDtypeStruct((2, PARTS, 3 * half, BLOCK), bf16),
        ],
        in_specs=[smem_spec()] + vmem_specs(9),
        out_specs=vmem_specs(2),
        scratch_shapes=[pltpu.VMEM((BLOCK, 2 * half), f32), pltpu.VMEM((BLOCK, half), f32)],
        compiler_params=params(),
        name="forward",
    )(table, got, *pairs, *downs)


def rows_body(table, cat_ref, *refs):
    pairs = refs[:4]
    out_ref, acc = refs[4:]
    width = acc.shape[2]
    per = BLOCK // ROWS

    def block(b, carry):
        for r in range(2):
            for n in (n for k in range(r, RING, 2) for n in (2 * k, 2 * k + 1)):
                part = dot(cat_ref[r, b], pair_of(pairs, n), contract_last)
                if r == 0:
                    acc[table[n]] = part
                else:
                    total = (acc[table[n]] + part).astype(bf16)
                    out_ref[pl.ds(b * per, per), table[n]] = total.reshape(per, ROWS, width)
        return carry

    lax.fori_loop(0, PARTS, block, 0)


def row_grads(table, cat, pairs):
    width = pairs[0].shape[2]
    return pl.pallas_call(
        rows_body,
        out_shape=jax.ShapeDtypeStruct((COLS, RING, ROWS, width), bf16),
        in_specs=[smem_spec()] + vmem_specs(5),
        out_specs=pl.BlockSpec(memory_space=pltpu.VMEM),
        scratch_shapes=[pltpu.VMEM((RING, BLOCK, width), f32)],
        compiler_params=params(),
        name="row_grads",
    )(table, cat, *pairs)


def terms_body(table, turn_ref, near_ref, far_ref, own_ref, other_ref):
    half = turn_ref.shape[2] // 3
    per = BLOCK // ROWS
    for out, ref in ((own_ref, near_ref), (other_ref, far_ref)):
        for n, part in enumerate((slice(0, 2 * half), slice(2 * half, 3 * half))):
            total = None
            for b in range(PARTS):
                right = ref[b * per : (b + 1) * per, 0, n * ROWS : (n + 1) * ROWS, :]
                product = dot(turn_ref[0, b, part, :], right.reshape(BLOCK, ref.shape[3]))
                total = product if total is None else total + product
            out[0, part, :] = total.astype(bf16)


def weight_terms(table, turn, got, steps):
    _, parts, triple, rows = turn.shape
    width = got.shape[3]
    at = [
        pl.BlockSpec((COLS, 1, 2 * ROWS, width), lambda g, t, j=j: (0, t[1 + j, g], 0, 0))
        for j in range(2)
    ]
    out = pl.BlockSpec((1, triple, width), lambda g, t: (g, 0, 0))
    shape = jax.ShapeDtypeStruct((len(steps), triple, width), bf16)
    own, other = pl.pallas_call(
        terms_body,
        out_shape=[shape, shape],
        grid_spec=pltpu.PrefetchScalarGridSpec(
            num_scalar_prefetch=1,
            grid=(len(steps),),
            in_specs=[pl.BlockSpec((1, parts, triple, rows), lambda g, t: (t[0, g], 0, 0, 0))] + at,
            out_specs=[out, out],
        ),
        compiler_params=params(),
        name="weight_terms",
    )(table, turn, got, got)
    return own, other


def adam_body(own, other, rise_pair, fall_pair, rise, fall, *refs):
    half = rise.shape[0]
    near = own[0].astype(f32) + other[0].astype(f32)
    far = (
        rise_pair[...].astype(f32) + fall_pair[...].astype(f32),
        rise[...].astype(f32) + fall[...].astype(f32),
    )
    gradients = (
        (near[0:half] + far[0][0:half]).T,
        (near[half : 2 * half] + far[0][half : 2 * half]).T,
        near[2 * half : 3 * half] + far[1],
    )
    for n, gradient in enumerate(gradients):
        w_ref, m_ref, v_ref = refs[3 * n : 3 * n + 3]
        w_out, m_out, v_out = refs[9 + 3 * n : 12 + 3 * n]
        weight = w_ref[0].astype(f32)
        first = beta_one * m_ref[0] + (1.0 - beta_one) * gradient
        second = beta_two * v_ref[0] + (1.0 - beta_two) * gradient * gradient
        update = (
            first / bias_one / (jnp.sqrt(second / bias_two) + epsilon) + decay_rate * weight
        )
        w_out[0] = (weight - learn_rate * update).astype(bf16)
        m_out[0] = first
        v_out[0] = second


def adam(own, other, pair_sums, down_sums, *state):
    lanes = 128
    triple, width = own.shape[1:]
    half = triple // 3
    near = pl.BlockSpec((1, triple, lanes), lambda g: (TERMS.index(0), 0, g))
    pair = pl.BlockSpec((2 * half, lanes), lambda g: (0, g))
    single = pl.BlockSpec((half, lanes), lambda g: (0, g))
    tall = pl.BlockSpec((1, lanes, half), lambda g: (0, g, 0))
    wide = pl.BlockSpec((1, half, lanes), lambda g: (0, 0, g))
    states = [tall] * 6 + [wide] * 3
    return pl.pallas_call(
        adam_body,
        grid=(width // lanes,),
        out_shape=[jax.ShapeDtypeStruct(v.shape, v.dtype) for v in state],
        in_specs=[near, near, pair, pair, single, single] + states,
        out_specs=states,
        compiler_params=params(),
        name="adam",
    )(own, other, *pair_sums, *down_sums, *state)


def gather_ring(own, reaches):
    chunks = [[None] * RING for _ in own]
    rising, falling = list(own), list(own)
    for m, piece in enumerate(own):
        chunks[m][0] = piece
    for step in range(1, RING):
        for m, reach in enumerate(reaches):
            if step <= reach:
                rising[m] = up_z(rising[m])
                chunks[m][RING - step] = rising[m]
            if step <= RING - 1 - reach:
                falling[m] = down_z(falling[m])
                chunks[m][step] = falling[m]
    groups = [[jnp.stack([chunk[k] for k in steps]) for steps in GROUPS] for chunk in chunks]
    return [[v for group in piece for v in (group, swap_core(group))] for piece in groups]


def ring_sum(own, other, k, part, carried=None):
    at = TERMS.index(k)
    if carried is None:
        return (own[at, part].astype(f32) + other[at, part].astype(f32)).astype(bf16)
    own, other, carried = lax.optimization_barrier((own, other, carried))
    total = own[at, part].astype(f32) + other[at, part].astype(f32) + carried.astype(f32)
    return total.astype(bf16)


def scatter_ring(own, other, parts, reaches):
    rising = [ring_sum(own, other, reach, part) for part, reach in zip(parts, reaches)]
    falling = [ring_sum(own, other, reach + 1, part) for part, reach in zip(parts, reaches)]
    for step in range(1, RING):
        for m, reach in reversed(list(enumerate(reaches))):
            if step <= reach:
                if step > 1:
                    k = reach - step + 1
                    rising[m] = ring_sum(own, other, k, parts[m], rising[m])
                rising[m] = up_z(rising[m])
            if step <= RING - 1 - reach:
                if step > 1:
                    k = reach + step
                    falling[m] = ring_sum(own, other, k, parts[m], falling[m])
                falling[m] = down_z(falling[m])
    return list(zip(rising, falling, strict=True))


def per_device(
    tokens,
    out_grad,
    expert_ids,
    gate_fixed,
    w_gate,
    w_up,
    w_down,
    m_gate,
    m_up,
    m_down,
    v_gate,
    v_up,
    v_down,
):
    zh, zl, core = lax.axis_index("zh"), lax.axis_index("zl"), lax.axis_index("c")
    rows = tokens.shape[0]
    half = w_gate.shape[2]

    def slices(steps):
        step = jnp.array(steps, jnp.int32)
        chip = (zh * 2 + zl + step) % RING
        return [step % 2] + [(chip // 2) * 2 + jnp.bitwise_xor(core, j) for j in range(2)]

    table = jnp.stack(slices(range(RING))[1:], axis=1).reshape(2 * RING).astype(jnp.int32)

    pick, sent = dispatch(
        expert_ids.reshape(1, rows), gate_fixed.reshape(1, rows), tokens, out_grad
    )
    (gate_own, up_own, down_own), sent = lax.optimization_barrier(((w_gate, w_up, w_down), sent))
    got = columns(sent)
    weights = (jnp.concatenate([gate_own, up_own], axis=0), down_own[0])
    pairs, downs = gather_ring(weights, REACH)
    cat, turn = forward(table, got, pairs, downs)

    at = jnp.stack(slices(TERMS)).astype(jnp.int32)
    own, other = weight_terms(at, turn, got, TERMS)
    cat, own, other = lax.optimization_barrier((cat, own, other))
    other = swap_core(other)
    pieces = row_grads(table, cat, pairs)
    back = columns(pieces)
    parts = (slice(0, 2 * half), slice(2 * half, 3 * half))
    sums = scatter_ring(own, other, parts, REACH)
    input_grad = combine(pick, back)
    states = (w_gate, m_gate, v_gate, w_up, m_up, v_up, w_down, m_down, v_down)
    new = adam(own, other, *sums, *states)
    return (input_grad,) + tuple(new[3 * m + i] for i in range(3) for m in range(3))


def solution(mesh):
    fine = Mesh(mesh.devices.reshape(4, 2, SIDE, SIDE, 2), ("zh", "c", "y", "x", "zl"))
    rows = P(("zh", "c", "y", "x", "zl"), None)
    tall = P(("y", "x", "zl"), ("zh", "c"), None)
    wide = P(("y", "x", "zl"), None, ("zh", "c"))
    states = (tall, tall, wide)
    return jax.shard_map(
        per_device,
        mesh=fine,
        in_specs=(rows,) * 4 + states * 3,
        out_specs=(rows,) + states * 3,
        check_vma=False,
    )
```
